32 devices in a mesh: head: 2 (over core), outer: 4 (over y, x), inner: 4 (over z).
Axes of the slice: x: 2, y: 2, z: 4, core: 2. Of those that a mesh axis runs over, the one named last changes fastest.
Arguments:
- queries: bfloat16 [8192, 2048], P(('outer', 'inner'), 'head'), may hold values from -6 to 6
- key_rows: bfloat16 [8192, 2048], P(('outer', 'inner'), 'head'), may hold values from -6 to 6
- value_rows: bfloat16 [8192, 2048], P(('outer', 'inner'), 'head'), may hold values from -6 to 6
- teacher_out: bfloat16 [8192, 2048], P(('outer', 'inner'), 'head'), may hold values from -6 to 6
- level_weights: bfloat16 [8, 8192], P(None, ('outer', 'inner')), may hold values from 0.125 to 1
Outputs:
- grad_queries: bfloat16 [8192, 2048], P(('outer', 'inner'), 'head')
- grad_keys: bfloat16 [8192, 2048], P(('outer', 'inner'), 'head')
- grad_values: bfloat16 [8192, 2048], P(('outer', 'inner'), 'head')
- grad_levels: float32 [8, 8192], P(None, ('outer', 'inner'))
The draws below stay inside these ranges and needn't reach their ends.
All inputs are finite; a program needn't handle non-finite values.
Results may differ from the reference program's by a relative error of at most 0.014.
Values may be sent and summed in bfloat16 or wider, within the bound.
No kernel may reach another device: no remote copies, remote signals or barrier semaphores. Data moves between devices by JAX's collectives and lax.ppermute only.
A program may use at most 128 MiB of HBM per device.

```python
import math
import jax
import jax.numpy as jnp
from jax import lax

TOK_DEV = 512
HEADS = 16
DK = 128
LEVELS = 8
SPANS = 16
TOKENS = 8192
BITS_IN = 2
BITS_OUT = 2
N_OUTER = 4
N_INNER = 4


def steps_of(rng, shape, cuts, least, high):
    def one(dim, parts):
        steps = jax.random.uniform(jax.random.fold_in(jax.random.fold_in(rng, 6), dim), (parts,), jnp.float32, least / len(cuts), high / len(cuts))
        return jnp.repeat(jnp.exp(steps), shape[dim] // parts).reshape((-1,) + (1,) * (len(shape) - dim - 1))

    factor_of = one(*cuts[0])
    for cut in cuts[1:]:
        factor_of = factor_of * one(*cut)
    return factor_of


def bell_draw(key, dims, spread, reach, split=(), kind=jnp.bfloat16):
    result = jax.random.normal(key, dims, jnp.float32) * spread
    if len(split) > 0:
        result = steps_of(key, dims, split, -0.22, 0.18) * result
    return jnp.clip(result, min=-reach, max=reach).astype(kind)


def setup_inputs(seed: int = 0) -> dict:
    key_of = jax.random.split(jax.random.key(seed), 6)
    queries = bell_draw(key_of[0], (TOKENS, HEADS * DK), 1.0, 6.0, ((0, 16), (1, 2)))
    key_rows = bell_draw(key_of[1], (TOKENS, HEADS * DK), 1.0, 6.0, ((0, 16), (1, 2)))
    value_rows = bell_draw(key_of[2], (TOKENS, HEADS * DK), 1.0, 6.0, ((0, 16), (1, 2)))
    teacher_out = bell_draw(key_of[3], (TOKENS, HEADS * DK), 1.0, 6.0, ((0, 16), (1, 2)))
    level_weights = jnp.clip(jnp.exp(math.log(1.0) - 2.0794415 * jax.random.uniform(key_of[4], (LEVELS, TOKENS), jnp.float32) ** steps_of(key_of[4], (LEVELS, TOKENS), ((1, 16),), -0.2, 0.2)), 0.125, 1.0).astype(jnp.bfloat16)
    return {"queries": queries, "key_rows": key_rows, "value_rows": value_rows, "teacher_out": teacher_out, "level_weights": level_weights}


HIGH = lax.Precision.HIGHEST


def bit_of(number, position):
    return (number >> position) % 2


def level_masks(block_id, forward):
    inner_pos = block_id % N_INNER
    group_pos = block_id // N_INNER
    members = jnp.arange(N_INNER, dtype=jnp.int32)
    groups_all = jnp.arange(N_OUTER, dtype=jnp.int32)
    own_bit = 1 if forward else 0
    rows_in = []
    rows_out = []
    for level_num in range(1, LEVELS):
        bit_pos = level_num - 1
        if bit_pos < BITS_IN:
            chosen = (bit_of(inner_pos, bit_pos) == own_bit) & ((members >> level_num) == (inner_pos >> level_num)) & (bit_of(members, bit_pos) == 1 - own_bit)
            rows_in.append(chosen)
            rows_out.append(jnp.zeros((N_OUTER,), dtype=bool))
        else:
            outer_bit = bit_pos - BITS_IN
            chosen = (bit_of(group_pos, outer_bit) == own_bit) & ((groups_all >> (outer_bit + 1)) == (group_pos >> (outer_bit + 1))) & (bit_of(groups_all, outer_bit) == 1 - own_bit)
            if outer_bit >= BITS_OUT:
                chosen = jnp.zeros((N_OUTER,), dtype=bool)
            rows_in.append(jnp.zeros((N_INNER,), dtype=bool))
            rows_out.append(chosen)
    return jnp.stack(rows_in).astype(jnp.float32), jnp.stack(rows_out).astype(jnp.float32)


def to_low(array):
    return lax.optimization_barrier(array.astype(jnp.bfloat16)).astype(jnp.float32)


def reference(queries, key_rows, value_rows, teacher_out, level_weights):
    gamma = DK ** -0.5
    scale_list = [TOK_DEV ** -0.5] + [gamma * (TOK_DEV * 2 ** (num - 1)) ** -0.5 for num in range(1, LEVELS)]
    scales = jnp.array(scale_list, dtype=jnp.float32)
    query_blocks = queries.reshape(SPANS, TOK_DEV, HEADS, DK)
    key_blocks = key_rows.reshape(SPANS, TOK_DEV, HEADS, DK)
    value_blocks = value_rows.reshape(SPANS, TOK_DEV, HEADS, DK)
    teacher_blocks = teacher_out.reshape(SPANS, TOK_DEV, HEADS, DK)
    weight_blocks = level_weights.reshape(LEVELS, SPANS, TOK_DEV).transpose(1, 0, 2)
    block_ids = jnp.arange(SPANS, dtype=jnp.int32)

    def state_of(index):
        keys32 = key_blocks[index].astype(jnp.float32)
        values32 = value_blocks[index].astype(jnp.float32)
        return jnp.einsum('thd,the->hde', keys32, values32).astype(jnp.bfloat16)

    block_states = lax.map(state_of, block_ids)
    group_totals = block_states.astype(jnp.float32).reshape(N_OUTER, N_INNER, HEADS, DK, DK).sum(axis=1).astype(jnp.bfloat16)
    totals32 = group_totals.astype(jnp.float32)
    positions = jnp.arange(TOK_DEV, dtype=jnp.int32)
    lower = positions[:, None] >= positions[None, :]

    def first_pass(index):
        in_mask, out_mask = level_masks(index, True)
        group_pos = index // N_INNER
        group_states = lax.dynamic_slice_in_dim(block_states, (group_pos * N_INNER).astype(jnp.int32), N_INNER, 0).astype(jnp.float32)
        level_state = jnp.einsum('lj,jhde->lhde', in_mask, group_states, precision=HIGH) + jnp.einsum('lg,ghde->lhde', out_mask, totals32, precision=HIGH)
        state32 = to_low(level_state)
        query32 = query_blocks[index].astype(jnp.float32)
        key32 = key_blocks[index].astype(jnp.float32)
        value32 = value_blocks[index].astype(jnp.float32)
        teacher32 = teacher_blocks[index].astype(jnp.float32)
        coefs = weight_blocks[index].astype(jnp.float32) * scales[:, None]
        scores = gamma * jnp.einsum('thd,shd->hts', query32, key32)
        scores32 = to_low(jnp.where(lower[None], scores, 0.0))
        intra = jnp.einsum('hts,she->the', scores32, value32)
        reads = jnp.einsum('thd,lhde->lthe', query32, state32)
        student = coefs[0][:, None, None] * intra + jnp.sum(coefs[1:, :, None, None] * reads, axis=0)
        error32 = to_low(student - teacher32)
        back_reads = jnp.einsum('the,lhde->lthd', error32, state32)
        grad_first = scales[0] * jnp.sum(error32 * intra, axis=(1, 2))
        grad_rest = scales[1:, None] * jnp.sum(query32[None] * back_reads, axis=(2, 3))
        grad_lv = jnp.concatenate([grad_first[None], grad_rest], axis=0)
        intra_err = to_low(coefs[0][:, None, None] * error32)
        score_grad = to_low(jnp.where(lower[None], gamma * jnp.einsum('the,she->hts', intra_err, value32), 0.0))
        grad_q = jnp.einsum('hts,shd->thd', score_grad, key32) + jnp.sum(coefs[1:, :, None, None] * back_reads, axis=0)
        exists = bit_of(index, jnp.arange(LEVELS - 1, dtype=jnp.int32)).astype(jnp.float32)
        weighted = to_low((coefs[1:] * exists[:, None])[:, :, None, None] * error32[None])
        adjoint = jnp.einsum('thd,lthe->lhde', query32, weighted)
        key_part = jnp.einsum('hts,thd->shd', score_grad, query32)
        value_part = jnp.einsum('hts,the->she', scores32, intra_err)
        return grad_q.astype(jnp.bfloat16), grad_lv, adjoint, key_part, value_part

    grad_q_all, grad_lv_all, adjoints, key_parts, value_parts = lax.map(first_pass, block_ids)
    group_adjoint = adjoints.reshape(N_OUTER, N_INNER, LEVELS - 1, HEADS, DK, DK).sum(axis=1)

    def second_pass(index):
        in_mask, out_mask = level_masks(index, False)
        group_pos = index // N_INNER
        group_adj = lax.dynamic_slice_in_dim(adjoints, (group_pos * N_INNER).astype(jnp.int32), N_INNER, 0)
        total = jnp.einsum('lj,jlhde->hde', in_mask, group_adj, precision=HIGH) + jnp.einsum('lg,glhde->hde', out_mask, group_adjoint, precision=HIGH)
        adjoint32 = to_low(total)
        key32 = key_blocks[index].astype(jnp.float32)
        value32 = value_blocks[index].astype(jnp.float32)
        grad_k = key_parts[index] + jnp.einsum('hde,she->shd', adjoint32, value32)
        grad_v = value_parts[index] + jnp.einsum('hde,shd->she', adjoint32, key32)
        return grad_k.astype(jnp.bfloat16), grad_v.astype(jnp.bfloat16)

    grad_k_all, grad_v_all = lax.map(second_pass, block_ids)
    grad_queries = grad_q_all.reshape(TOKENS, HEADS * DK)
    grad_keys = grad_k_all.reshape(TOKENS, HEADS * DK)
    grad_values = grad_v_all.reshape(TOKENS, HEADS * DK)
    grad_levels = grad_lv_all.transpose(1, 0, 2).reshape(LEVELS, TOKENS)
    return grad_queries, grad_keys, grad_values, grad_levels
```

```python
import functools

import jax
import jax.numpy as jnp
from jax import lax
from jax.experimental import pallas as pl
from jax.experimental.pallas import tpu as pltpu
from jax.sharding import PartitionSpec as P

DK = 128
LEVELS = 8
CHUNKS = 2

F32 = jnp.float32
BF16 = jnp.bfloat16


def mm(a, b):
    return lax.dot_general(a, b, (((1,), (0,)), ((), ())), preferred_element_type=F32)


def mm_nt(a, b):
    return lax.dot_general(a, b, (((1,), (1,)), ((), ())), preferred_element_type=F32)


def mm_tn(a, b):
    return lax.dot_general(a, b, (((0,), (0,)), ((), ())), preferred_element_type=F32)


def lower_mask(rows):
    t = lax.broadcasted_iota(jnp.int32, (rows, rows), 0)
    s = lax.broadcasted_iota(jnp.int32, (rows, rows), 1)
    return t >= s


def swap(value, axis, mask):
    pairs = [(source, source ^ mask) for source in range(lax.axis_size(axis))]
    return lax.ppermute(value, axis, pairs)


def cost(flops, nbytes):
    return pl.CostEstimate(flops=flops, transcendentals=0, bytes_accessed=nbytes)


def columns(rows, first):
    return pl.BlockSpec((rows, DK), lambda h: (0, h + first))


def per_head(*shape):
    return pl.BlockSpec((None,) + shape, lambda h: (h,) + (0,) * len(shape))


def whole(*shape):
    return pl.BlockSpec(shape, lambda h: (0,) * len(shape))


SMEM = pl.BlockSpec(memory_space=pltpu.SMEM)


def state_kernel(key_ref, value_ref, state_ref):
    state_ref[...] = mm_tn(key_ref[...], value_ref[...]).astype(BF16)


def intra_kernel(gamma, count, query_ref, key_ref, value_ref, col_ref, row_ref, score_ref, intra_ref, wide_ref, tall_ref):
    rows = query_ref.shape[0]
    query = query_ref[...]
    scores = gamma * mm_nt(query, key_ref[...])
    low = jnp.where(lower_mask(rows), scores, 0.0).astype(BF16)
    score_ref[...] = low
    intra_ref[...] = mm(low, value_ref[...])
    query32 = query.astype(F32)
    turned = query32.T
    for num in range(count):
        wide_ref[:, num * DK : (num + 1) * DK] = (query32 * col_ref[:, num + 1 : num + 2]).astype(BF16)
        tall_ref[num * DK : (num + 1) * DK, :] = (turned * row_ref[num + 1 : num + 2, :]).astype(BF16)


def error_kernel(count, bits_ref, wide_ref, tall_ref, intra_ref, col_ref, teacher_ref, *refs):
    states, error_ref, adjoints = refs[:count], refs[count], refs[count + 1 :]
    low = jnp.concatenate(
        [jnp.where(bits_ref[num] == 1, states[num][...], jnp.zeros((DK, DK), BF16)) for num in range(count)], axis=0
    )
    student = col_ref[:, 0:1] * intra_ref[...] + mm(wide_ref[...], low)
    error = (student - teacher_ref[...].astype(F32)).astype(BF16)
    error_ref[...] = error
    adjoint = mm(tall_ref[...], error)
    for num in range(count):
        part = adjoint[num * DK : (num + 1) * DK]
        adjoints[num][...] = jnp.where(bits_ref[num] == 1, part, 0.0).astype(adjoints[num].dtype)


def grad_kernel(gamma, count, heads, bits_ref, query_ref, key_ref, value_ref, error_ref, score_ref, intra_ref, col_ref, *refs):
    states = refs[:count]
    gq_ref, gk_ref, gv_ref, gl_ref, acc = refs[-5:]
    head = pl.program_id(0)
    rows = query_ref.shape[0]
    query, key, value, error = query_ref[...], key_ref[...], value_ref[...], error_ref[...]
    error32 = error.astype(F32)
    query32 = query.astype(F32)

    @pl.when(head == 0)
    def _():
        acc[...] = jnp.zeros_like(acc)

    acc[0] += error32 * intra_ref[...]
    inner = (col_ref[:, 0:1] * error32).astype(BF16)
    raw = gamma * mm_nt(inner, value)
    slope = jnp.where(lower_mask(rows), raw, 0.0).astype(BF16)
    total = mm(slope, key)
    for num in range(count):
        state = jnp.where(bits_ref[num] == 1, states[num][...], jnp.zeros((DK, DK), BF16))
        back = mm_nt(error, state)
        acc[num + 1] += query32 * back
        total += col_ref[:, num + 1 : num + 2] * back
    gq_ref[...] = total.astype(BF16)
    gk_ref[...] = mm_tn(slope, query)
    gv_ref[...] = mm_tn(score_ref[...], inner)

    @pl.when(head == heads - 1)
    def _():
        gl_ref[...] = jnp.zeros_like(gl_ref)
        ones = jnp.ones((8, DK), F32)
        for num in range(count + 1):
            line = lax.dot_general(
                ones, acc[num], (((1,), (1,)), ((), ())), preferred_element_type=F32, precision=lax.Precision.HIGHEST
            )
            gl_ref[num : num + 1, :] = line[0:1]


def final_kernel(count, key_ref, value_ref, gk_ref, gv_ref, *refs):
    parts = refs[:count]
    outk_ref, outv_ref = refs[-2:]
    total = parts[0][...].astype(F32)
    for part in parts[1:]:
        total += part[...].astype(F32)
    adjoint = total.astype(BF16)
    outk_ref[...] = (gk_ref[...] + mm_nt(value_ref[...], adjoint)).astype(BF16)
    outv_ref[...] = (gv_ref[...] + mm(key_ref[...], adjoint)).astype(BF16)


def on_device(queries, key_rows, value_rows, teacher_out, level_weights):
    rows, width = queries.shape
    heads = width // DK
    inner_count = lax.axis_size("inner")
    outer_count = lax.axis_size("outer")
    inner_bits = inner_count.bit_length() - 1
    outer_bits = outer_count.bit_length() - 1
    count = inner_bits + outer_bits
    gamma = DK ** (-0.5)
    scale_list = [rows ** (-0.5)] + [gamma * (rows * 2 ** (num - 1)) ** (-0.5) for num in range(1, LEVELS)]
    scales = jnp.array(scale_list, dtype=F32)
    block = lax.axis_index("outer") * inner_count + lax.axis_index("inner")
    bits = (block >> jnp.arange(count, dtype=jnp.int32)) % 2
    row_coefs = level_weights.astype(F32) * scales[:, None]
    col_coefs = row_coefs.T

    moves = [("inner", 2 ** (bit + 1) - 1) for bit in range(inner_bits)]
    moves += [("outer", 2**bit) for bit in range(outer_bits)]
    size = heads // CHUNKS
    chunks = range(CHUNKS)
    mat = DK * DK
    flop = 2 * rows * mat

    def state_call(first):
        return pl.pallas_call(
            state_kernel,
            grid=(size,),
            in_specs=[columns(rows, first)] * 2,
            out_specs=per_head(DK, DK),
            out_shape=jax.ShapeDtypeStruct((size, DK, DK), BF16),
            cost_estimate=cost(size * flop, size * 4 * rows * DK),
            name="state",
        )(key_rows, value_rows)

    def intra_call(first):
        return pl.pallas_call(
            functools.partial(intra_kernel, gamma, count),
            grid=(size,),
            in_specs=[columns(rows, first)] * 3 + [whole(rows, LEVELS), whole(LEVELS, rows)],
            out_specs=[per_head(rows, rows), per_head(rows, DK), per_head(rows, count * DK), per_head(count * DK, rows)],
            out_shape=[
                jax.ShapeDtypeStruct((size, rows, rows), BF16),
                jax.ShapeDtypeStruct((size, rows, DK), F32),
                jax.ShapeDtypeStruct((size, rows, count * DK), BF16),
                jax.ShapeDtypeStruct((size, count * DK, rows), BF16),
            ],
            cost_estimate=cost(size * 12 * flop, size * rows * (6 * DK + 4 * DK + 2 * rows)),
            name="intra",
        )(queries, key_rows, value_rows, col_coefs, row_coefs)

    def error_call(first, pre, states):
        score, intra, wide, tall = pre
        return pl.pallas_call(
            functools.partial(error_kernel, count),
            grid=(size,),
            in_specs=[
                SMEM,
                per_head(rows, count * DK),
                per_head(count * DK, rows),
                per_head(rows, DK),
                whole(rows, LEVELS),
                columns(rows, first),
            ]
            + [per_head(DK, DK)] * count,
            out_specs=[per_head(rows, DK)] + [per_head(DK, DK)] * count,
            out_shape=[jax.ShapeDtypeStruct((size, rows, DK), BF16)]
            + [jax.ShapeDtypeStruct((size, DK, DK), F32)] * (count - 1)
            + [jax.ShapeDtypeStruct((size, DK, DK), BF16)],
            cost_estimate=cost(size * 8 * flop, size * rows * DK * 8),
            name="error",
        )(bits, wide, tall, intra, col_coefs, teacher_out, *states)

    def grad_call(first, pre, states, error, earlier):
        score, intra, wide, tall = pre
        args = [bits, queries, key_rows, value_rows, error, score, intra, col_coefs, *states]
        specs = [SMEM] + [columns(rows, first)] * 3
        specs += [per_head(rows, DK), per_head(rows, rows), per_head(rows, DK), whole(rows, LEVELS)]
        specs += [per_head(DK, DK)] * count
        alias = {}
        if earlier is not None:
            alias = {len(args): 0}
            args.append(earlier)
            specs.append(pl.BlockSpec(memory_space=pl.ANY))
        return pl.pallas_call(
            functools.partial(grad_kernel, gamma, count, size),
            grid=(size,),
            in_specs=specs,
            out_specs=[columns(rows, first), per_head(rows, DK), per_head(rows, DK), whole(LEVELS, rows)],
            out_shape=[
                jax.ShapeDtypeStruct((rows, width), BF16),
                jax.ShapeDtypeStruct((size, rows, DK), F32),
                jax.ShapeDtypeStruct((size, rows, DK), F32),
                jax.ShapeDtypeStruct((LEVELS, rows), F32),
            ],
            scratch_shapes=[pltpu.VMEM((count + 1, rows, DK), F32)],
            input_output_aliases=alias,
            cost_estimate=cost(size * 24 * flop, size * rows * (24 * DK + 2 * rows)),
            name="grad",
        )(*args)

    def final_call(first, partk, partv, parts, earlier):
        args = [key_rows, value_rows, partk, partv, *parts]
        specs = [columns(rows, first)] * 2 + [per_head(rows, DK)] * 2 + [per_head(DK, DK)] * count
        alias = {}
        if earlier is not None:
            alias = {len(args): 0, len(args) + 1: 1}
            args += list(earlier)
            specs += [pl.BlockSpec(memory_space=pl.ANY)] * 2
        return pl.pallas_call(
            functools.partial(final_kernel, count),
            grid=(size,),
            in_specs=specs,
            out_specs=[columns(rows, first)] * 2,
            out_shape=[jax.ShapeDtypeStruct((rows, width), BF16)] * 2,
            input_output_aliases=alias,
            cost_estimate=cost(size * 2 * flop, size * rows * DK * 16),
            name="final",
        )(*args)

    own = [state_call(c * size) for c in chunks]
    pre = [intra_call(c * size) for c in chunks]
    states = [[] for c in chunks]
    for axis, mask in moves:
        for c in chunks:
            running = own[c].astype(F32)
            for received in states[c]:
                running = running + received.astype(F32)
            states[c].append(swap(running.astype(BF16), axis, mask))
    errors, adjoints = [], []
    for c in chunks:
        error, *adjoint = error_call(c * size, pre[c], states[c])
        errors.append(error)
        adjoints.append(adjoint)
    parts = [[] for c in chunks]
    for num in reversed(range(count)):
        axis, mask = moves[num]
        for c in chunks:
            running = adjoints[c][num].astype(F32)
            for received in parts[c]:
                running = running + received.astype(F32)
            parts[c].append(swap(running.astype(BF16), axis, mask))
    grad_queries, level_lines, local = None, None, []
    for c in chunks:
        grad_queries, partk, partv, lines = grad_call(c * size, pre[c], states[c], errors[c], grad_queries)
        local.append((partk, partv))
        level_lines = lines if level_lines is None else level_lines + lines
    level_lines = level_lines * scales[:, None]
    grad_levels = level_lines
    for shift in range(1, lax.axis_size("head")):
        pairs = [(s, (s + shift) % lax.axis_size("head")) for s in range(lax.axis_size("head"))]
        grad_levels = grad_levels + lax.ppermute(level_lines, "head", pairs)
    outs = None
    for c in chunks:
        outs = final_call(c * size, *local[c], parts[c], outs)
    return (grad_queries, outs[0], outs[1], grad_levels)


def solution(mesh):
    rows = P(("outer", "inner"), "head")
    level = P(None, ("outer", "inner"))
    return jax.shard_map(
        on_device,
        mesh=mesh,
        in_specs=(rows, rows, rows, rows, level),
        out_specs=(rows, rows, rows, level),
        check_vma=False,
    )
```

```python
import functools

import jax
import jax.numpy as jnp
from jax import lax
from jax.experimental import pallas as pl
from jax.experimental.pallas import tpu as pltpu
from jax.sharding import PartitionSpec as P


DK = 128
LEVELS = 8
CHUNKS = 2
PIECES = 2

F32 = jnp.float32
BF16 = jnp.bfloat16


def mm(a, b):
    return lax.dot_general(a, b, (((1,), (0,)), ((), ())), preferred_element_type=F32)


def mm_nt(a, b):
    return lax.dot_general(a, b, (((1,), (1,)), ((), ())), preferred_element_type=F32)


def mm_tn(a, b):
    return lax.dot_general(a, b, (((0,), (0,)), ((), ())), preferred_element_type=F32)


def lower_mask(rows):
    t = lax.broadcasted_iota(jnp.int32, (rows, rows), 0)
    s = lax.broadcasted_iota(jnp.int32, (rows, rows), 1)
    return t >= s


def swap(value, axis, mask):
    pairs = [(source, source ^ mask) for source in range(lax.axis_size(axis))]
    return lax.ppermute(value, axis, pairs)


def cost(flops, nbytes):
    return pl.CostEstimate(flops=flops, transcendentals=0, bytes_accessed=nbytes)


SMEM = pl.BlockSpec(memory_space=pltpu.SMEM)
VMEM = pl.BlockSpec(memory_space=pltpu.VMEM)
HBM = pl.BlockSpec(memory_space=pltpu.HBM)


def head_columns(head):
    return slice(head * DK, (head + 1) * DK)


def masked_states(bits_ref, states, head):
    return [
        jnp.where(bits_ref[num] == 1, state[head], jnp.zeros((DK, DK), BF16)) for num, state in enumerate(states)
    ]


def state_kernel(first, size, key_in, value_in, state_ref, key_ref, value_ref, sent_ref, sems):
    copies = []
    for head in range(size):
        for num, (source, kept) in enumerate(((key_in, key_ref), (value_in, value_ref))):
            copy = pltpu.make_async_copy(source.at[:, head_columns(first + head)], kept.at[head], sems.at[num, head])
            copy.start()
            copies.append(copy)
    for head in range(size):
        copies[2 * head].wait()
        copies[2 * head + 1].wait()
        state = mm_tn(key_ref[head], value_ref[head]).astype(BF16)
        state_ref[head] = state
        sent_ref[head] = state


def load_heads(source, kept, sems, heads):
    copies = [pltpu.make_async_copy(source.at[:, head_columns(h)], kept.at[h], sems.at[h]) for h in range(heads)]
    for copy in copies:
        copy.start()
    return copies


def intra_kernel(gamma, scale_list, count, first, size, heads, lead, *refs):
    if lead:
        key_ref, value_ref, level_ref, query_in = refs[:4]
        score_ref, intra_ref, wide_ref, tall_ref, query_ref, coef_ref, sems = refs[4:]
        copies = load_heads(query_in, query_ref, sems, heads)
        rows = level_ref.shape[1]
        place = lax.broadcasted_iota(jnp.int32, (LEVELS, 1), 0)
        scale = jnp.zeros((LEVELS, 1), F32)
        for num, number in enumerate(scale_list):
            scale = jnp.where(place == num, number, scale)
        coefs = level_ref[...].astype(F32) * scale
        turned_coefs = coefs.T
        for num in range(count + 1):
            coef_ref[num] = jnp.broadcast_to(turned_coefs[:, num : num + 1], (rows, DK))
    else:
        key_ref, value_ref, query_ref, coef_ref, teacher_in = refs[:5]
        score_ref, intra_ref, wide_ref, tall_ref, teacher_ref, sems = refs[5:]
        copies = load_heads(teacher_in, teacher_ref, sems, heads)
        rows = query_ref.shape[1]
    for head in range(size):
        if lead:
            copies[head].wait()
        query, key = query_ref[first + head], key_ref[head]
        low = jnp.where(lower_mask(rows), gamma * mm_nt(query, key), 0.0).astype(BF16)
        score_ref[head] = low.T
        intra_ref[head] = mm(low, value_ref[head])
        query32 = query.astype(F32)
        for num in range(count):
            wide = (query32 * coef_ref[num + 1]).astype(BF16)
            wide_ref[head, :, num * DK : (num + 1) * DK] = wide
            tall_ref[head, num * DK : (num + 1) * DK, :] = wide.T
    for copy in copies[size:] if lead else copies:
        copy.wait()


def error_kernel(count, first, size, bits_ref, wide_ref, tall_ref, intra_ref, coef_ref, teacher_ref, *refs):
    states, error_ref, adjoints = refs[:count], refs[count], refs[count + 1 :]
    for head in range(size):
        low = jnp.concatenate(masked_states(bits_ref, states, head), axis=0)
        student = coef_ref[0] * intra_ref[head] + mm(wide_ref[head], low)
        error = (student - teacher_ref[first + head].astype(F32)).astype(BF16)
        error_ref[head] = error
        adjoint = mm(tall_ref[head], error)
        for num in range(count):
            part = adjoint[num * DK : (num + 1) * DK]
            adjoints[num][head] = jnp.where(bits_ref[num] == 1, part, 0.0).astype(adjoints[num].dtype)


def grad_kernel(gamma, scale_list, count, first, skip, size, bits_ref, query_ref, key_ref, value_ref, error_ref, score_ref, intra_ref, coef_ref, *refs):
    states = refs[:count]
    outq_ref, gk_ref, gv_ref, gl_ref, acc, kept, sems = refs[-7:]
    rows = query_ref.shape[1]
    copies = []
    for place in range(size):
        head = skip + place
        cols = head_columns(first + head)
        query, key, value, error = query_ref[first + head], key_ref[head], value_ref[head], error_ref[head]
        error32 = error.astype(F32)
        query32 = query.astype(F32)
        inner = (coef_ref[0] * error32).astype(BF16)
        slope = jnp.where(lower_mask(rows), gamma * mm_nt(inner, value), 0.0).astype(BF16)
        total = mm(slope, key)
        back = mm_nt(error, jnp.concatenate(masked_states(bits_ref, states, head), axis=0))
        terms = [error32 * intra_ref[head]]
        for num in range(count):
            part = back[:, num * DK : (num + 1) * DK]
            terms.append(query32 * part)
            total += coef_ref[num + 1] * part
        for num, term in enumerate(terms):
            if place == 0:
                acc[num] = term
            else:
                acc[num] += term
        kept[place] = total.astype(BF16)
        copies.append(pltpu.make_async_copy(kept.at[place], outq_ref.at[:, cols], sems.at[place]))
        copies[-1].start()
        gk_ref[place] = mm_tn(slope, query)
        gv_ref[place] = mm(score_ref[head], inner)
    gl_ref[...] = jnp.zeros_like(gl_ref)
    for num in range(count + 1):
        gl_ref[num : num + 1, :] = scale_list[num] * jnp.sum(acc[num].T, axis=0, keepdims=True)
    for copy in copies:
        copy.wait()


def final_kernel(count, first, size, pieces, lines, key_ref, value_ref, *refs):
    span = size // pieces
    line_refs, refs = refs[:lines], refs[lines:]
    partk, partv, parts = refs[:pieces], refs[pieces : 2 * pieces], refs[2 * pieces : 2 * pieces + count]
    copies = []
    if lines:
        *refs, line_out, kept_k, kept_v, sems, line_kept, line_sem = refs
        line_kept[...] = sum((part[...] for part in line_refs[1:]), line_refs[0][...])
        copies.append(pltpu.make_async_copy(line_kept, line_out, line_sem))
        copies[0].start()
    else:
        *refs, kept_k, kept_v, sems = refs
    outk_ref, outv_ref = refs[-2:]
    for head in range(size):
        cols = head_columns(first + head)
        total = parts[0][head].astype(F32)
        for part in parts[1:]:
            total += part[head].astype(F32)
        adjoint = total.astype(BF16)
        piece, place = head // span, head % span
        kept_k[head] = (partk[piece][place] + mm_nt(value_ref[head], adjoint)).astype(BF16)
        kept_v[head] = (partv[piece][place] + mm(key_ref[head], adjoint)).astype(BF16)
        for num, (kept, out) in enumerate(((kept_k, outk_ref), (kept_v, outv_ref))):
            copies.append(pltpu.make_async_copy(kept.at[head], out.at[:, cols], sems.at[num, head]))
            copies[-1].start()
    for copy in copies:
        copy.wait()


def on_device(queries, key_rows, value_rows, teacher_out, level_weights):
    rows, width = queries.shape
    heads = width // DK
    inner_count = lax.axis_size("inner")
    outer_count = lax.axis_size("outer")
    inner_bits = inner_count.bit_length() - 1
    outer_bits = outer_count.bit_length() - 1
    count = inner_bits + outer_bits
    gamma = DK ** (-0.5)
    scale_list = [rows ** (-0.5)] + [gamma * (rows * 2 ** (num - 1)) ** (-0.5) for num in range(1, LEVELS)]
    block = lax.axis_index("outer") * inner_count + lax.axis_index("inner")
    bits = (block >> jnp.arange(count, dtype=jnp.int32)) % 2

    moves = [("inner", 2 ** (bit + 1) - 1) for bit in range(inner_bits)]
    moves += [("outer", 2**bit) for bit in range(outer_bits)]
    size = heads // CHUNKS
    span = size // PIECES
    chunks = range(CHUNKS)
    mat = DK * DK
    flop = 2 * rows * mat

    def arr(*shape, dtype=BF16):
        return jax.ShapeDtypeStruct(shape, dtype)

    def params(grant):
        return pltpu.CompilerParams(vmem_limit_bytes=grant * 2**20)

    def state_call(first):
        return pl.pallas_call(
            functools.partial(state_kernel, first, size),
            in_specs=[HBM] * 2,
            out_specs=[VMEM] * 4,
            out_shape=[arr(size, DK, DK), arr(size, rows, DK), arr(size, rows, DK), arr(size, DK, DK)],
            scratch_shapes=[pltpu.SemaphoreType.DMA((2, size))],
            compiler_params=params(2),
            cost_estimate=cost(size * flop, size * 4 * rows * DK),
            name="state",
        )(key_rows, value_rows)

    def intra_call(first, key, value, earlier):
        shapes = [
            arr(size, rows, rows),
            arr(size, rows, DK, dtype=F32),
            arr(size, rows, count * DK),
            arr(size, count * DK, rows),
            arr(heads, rows, DK),
        ]
        if earlier is None:
            args, specs = [key, value, level_weights, queries], [VMEM] * 3 + [HBM]
            shapes.append(arr(count + 1, rows, DK, dtype=F32))
        else:
            args, specs = [key, value, *earlier, teacher_out], [VMEM] * 4 + [HBM]
        return pl.pallas_call(
            functools.partial(intra_kernel, gamma, scale_list, count, first, size, heads, earlier is None),
            in_specs=specs,
            out_specs=[VMEM] * len(shapes),
            out_shape=shapes,
            scratch_shapes=[pltpu.SemaphoreType.DMA((heads,))],
            compiler_params=params(12),
            cost_estimate=cost(size * 12 * flop, size * rows * (6 * DK + 4 * DK + 2 * rows)),
            name="intra",
        )(*args)

    def error_call(first, pre, states):
        _, intra, wide, tall = pre
        return pl.pallas_call(
            functools.partial(error_kernel, count, first, size),
            in_specs=[SMEM] + [VMEM] * (5 + count),
            out_specs=[VMEM] * (1 + count),
            out_shape=[arr(size, rows, DK)]
            + [arr(size, DK, DK, dtype=F32)] * (count - 1)
            + [arr(size, DK, DK)],
            compiler_params=params(8),
            cost_estimate=cost(size * 8 * flop, size * rows * DK * 8),
            name="error",
        )(bits, wide, tall, intra, coef, teacher, *states)

    def grad_call(first, skip, key, value, pre, states, error, earlier):
        score, intra, _, _ = pre
        args = [bits, query, key, value, error, score, intra, coef, *states]
        specs = [SMEM] + [VMEM] * (len(args) - 1)
        alias = {}
        if earlier is not None:
            alias = {len(args): 0}
            args.append(earlier)
            specs.append(HBM)
        return pl.pallas_call(
            functools.partial(grad_kernel, gamma, scale_list, count, first, skip, span),
            in_specs=specs,
            out_specs=[HBM] + [VMEM] * 3,
            out_shape=[
                arr(rows, width),
                arr(span, rows, DK, dtype=F32),
                arr(span, rows, DK, dtype=F32),
                arr(LEVELS, rows, dtype=F32),
            ],
            scratch_shapes=[
                pltpu.VMEM((count + 1, rows, DK), F32),
                pltpu.VMEM((span, rows, DK), BF16),
                pltpu.SemaphoreType.DMA((span,)),
            ],
            input_output_aliases=alias,
            compiler_params=params(12),
            cost_estimate=cost(span * 24 * flop, span * rows * (24 * DK + 2 * rows)),
            name="grad",
        )(*args)

    def final_call(first, key, value, partk, partv, parts, earlier, lines):
        args = [key, value, *lines, *partk, *partv, *parts]
        specs = [VMEM] * len(args)
        shapes = [arr(rows, width)] * 2
        scratch = [pltpu.VMEM((size, rows, DK), BF16)] * 2 + [pltpu.SemaphoreType.DMA((2, size))]
        alias = {}
        if earlier is not None:
            alias = {len(args) + num: num for num in range(2)}
            args += list(earlier)
            specs += [HBM] * 2
        if lines:
            shapes.append(arr(LEVELS, rows, dtype=F32))
            scratch += [pltpu.VMEM((LEVELS, rows), F32), pltpu.SemaphoreType.DMA]
        return pl.pallas_call(
            functools.partial(final_kernel, count, first, size, len(partk), len(lines)),
            in_specs=specs,
            out_specs=[HBM] * len(shapes),
            out_shape=shapes,
            scratch_shapes=scratch,
            input_output_aliases=alias,
            compiler_params=params(4),
            cost_estimate=cost(size * 2 * flop, size * rows * DK * 16),
            name="final",
        )(*args)

    queries, key_rows, value_rows, teacher_out = [
        pltpu.with_memory_space_constraint(a, pltpu.HBM) for a in (queries, key_rows, value_rows, teacher_out)
    ]
    own, pre = [], []
    for c in chunks:
        own.append(state_call(c * size))
    for c in chunks:
        early = intra_call(c * size, *own[c][1:3], None if c == 0 else (query, coef))
        pre.append(early[:4])
        if c == 0:
            query, coef = early[4:]
        else:
            teacher = early[4]
    states = [[] for c in chunks]
    for step, (axis, mask) in enumerate(moves):
        for c in chunks:
            sent = own[c][3]
            if step > 0:
                sent = sum((a.astype(F32) for a in states[c]), own[c][0].astype(F32)).astype(BF16)
            states[c].append(swap(sent, axis, mask))
    errors, adjoints = [], []
    for c in chunks:
        error, *adjoint = error_call(c * size, pre[c], states[c])
        errors.append(error)
        adjoints.append(adjoint)
    parts = [[] for c in chunks]
    for num in reversed(range(count)):
        axis, mask = moves[num]
        for c in chunks:
            running = adjoints[c][num].astype(F32)
            for received in parts[c]:
                running = running + received.astype(F32)
            parts[c].append(swap(running.astype(BF16), axis, mask))
    grad_queries, level_lines, local = None, None, []
    for c in chunks:
        partk, partv = [], []
        for piece in range(PIECES):
            grad_queries, onek, onev, lines = grad_call(
                c * size, piece * span, *own[c][1:3], pre[c], states[c], errors[c], grad_queries
            )
            partk.append(onek)
            partv.append(onev)
            level_lines = lines if level_lines is None else level_lines + lines
        local.append((partk, partv))
    line_parts = [level_lines]
    head_count = lax.axis_size("head")
    for shift in range(1, head_count):
        pairs = [(source, (source + shift) % head_count) for source in range(head_count)]
        line_parts.append(lax.ppermute(level_lines, "head", pairs))
    outs = None
    for c in chunks:
        last = line_parts if c == CHUNKS - 1 else []
        outs = final_call(c * size, *own[c][1:3], *local[c], parts[c], outs, last)
    return (grad_queries, *outs)


def solution(mesh):
    rows = P(("outer", "inner"), "head")
    level = P(None, ("outer", "inner"))
    return jax.shard_map(
        on_device,
        mesh=mesh,
        in_specs=(rows, rows, rows, rows, level),
        out_specs=(rows, rows, rows, level),
        check_vma=False,
    )
```

```python
import functools

import jax
import jax.numpy as jnp
from jax import lax
from jax.experimental import pallas as pl
from jax.experimental.pallas import tpu as pltpu
from jax.sharding import PartitionSpec as P


DK = 128
LEVELS = 8
CHUNKS = 2
PIECES = (2, 2)

F32 = jnp.float32
BF16 = jnp.bfloat16


def mm(a, b):
    return lax.dot_general(a, b, (((1,), (0,)), ((), ())), preferred_element_type=F32)


def mm_nt(a, b):
    return lax.dot_general(a, b, (((1,), (1,)), ((), ())), preferred_element_type=F32)


def mm_tn(a, b):
    return lax.dot_general(a, b, (((0,), (0,)), ((), ())), preferred_element_type=F32)


def lower_scale(rows, gamma):
    t = lax.broadcasted_iota(jnp.int32, (rows, rows), 0)
    s = lax.broadcasted_iota(jnp.int32, (rows, rows), 1)
    return jnp.where(t >= s, gamma, 0.0)


def swap(value, axis, mask):
    pairs = [(source, source ^ mask) for source in range(lax.axis_size(axis))]
    return lax.ppermute(value, axis, pairs)


def cost(flops, nbytes):
    return pl.CostEstimate(flops=flops, transcendentals=0, bytes_accessed=nbytes)


VMEM = pl.BlockSpec(memory_space=pltpu.VMEM)
HBM = pl.BlockSpec(memory_space=pltpu.HBM)


def head_columns(head):
    return slice(head * DK, (head + 1) * DK)


def level_bits(count):
    block = lax.axis_index("outer") * lax.axis_size("inner") + lax.axis_index("inner")
    return [(block >> num) % 2 for num in range(count)]


def state_kernel(first, size, heads, *refs):
    copies, extra = [], []
    if first == 0:
        key_in, value_in, state_ref, key_ref, value_ref, sent_ref, sems = refs
    else:
        key_in, value_in, query_in, state_ref, key_ref, value_ref, sent_ref, query_ref, sems, query_sems = refs
    for head in range(size):
        for num, (source, kept) in enumerate(((key_in, key_ref), (value_in, value_ref))):
            copy = pltpu.make_async_copy(source.at[:, head_columns(first + head)], kept.at[head], sems.at[num, head])
            copy.start()
            copies.append(copy)
    if first > 0:
        extra = load_heads(query_in, query_ref, query_sems, heads)
    for head in range(size):
        copies[2 * head].wait()
        copies[2 * head + 1].wait()
        state = mm_tn(key_ref[head], value_ref[head]).astype(BF16)
        state_ref[head] = state
        sent_ref[head] = state
    for copy in extra:
        copy.wait()


def load_heads(source, kept, sems, heads):
    copies = [pltpu.make_async_copy(source.at[:, head_columns(h)], kept.at[h], sems.at[h]) for h in range(heads)]
    for copy in copies:
        copy.start()
    return copies


def intra_kernel(gamma, scale_list, count, first, size, heads, lead, *refs):
    if lead:
        key_ref, value_ref, level_ref, query_ref = refs[:4]
        score_ref, intra_ref, turned_ref, wide_ref, coef_ref, sems = refs[4:]
        copies = []
        rows = level_ref.shape[1]
        place = lax.broadcasted_iota(jnp.int32, (LEVELS, 1), 0)
        scale = jnp.zeros((LEVELS, 1), F32)
        for num, number in enumerate(scale_list):
            scale = jnp.where(place == num, number, scale)
        coefs = level_ref[...].astype(F32) * scale
        for num, bit in enumerate(level_bits(count)):
            coefs = jnp.where((place == num + 1) & (bit == 0), 0.0, coefs)
        turned_coefs = coefs.T
        for num in range(count + 1):
            coef_ref[num] = jnp.broadcast_to(turned_coefs[:, num : num + 1], (rows, DK))
    else:
        key_ref, value_ref, query_ref, coef_ref, teacher_in = refs[:5]
        score_ref, intra_ref, turned_ref, wide_ref, teacher_ref, sems = refs[5:]
        copies = load_heads(teacher_in, teacher_ref, sems, heads)
        rows = query_ref.shape[1]
    half = rows // 2
    upper, lower = slice(0, half), slice(half, rows)
    mask = lower_scale(half, gamma)
    for head in range(size):
        query, key, value = query_ref[first + head], key_ref[head], value_ref[head]
        turned_ref[head] = query.T
        query32 = query.astype(F32)
        for num in range(count):
            wide_ref[head, :, num * DK : (num + 1) * DK] = (query32 * coef_ref[num + 1]).astype(BF16)
        top = (mask * mm_nt(query[upper], key[upper])).astype(BF16)
        wide = mm_nt(query[lower], key)
        low = jnp.concatenate([gamma * wide[:, upper], mask * wide[:, lower]], axis=1).astype(BF16)
        score_ref[head, upper, upper] = top.T
        score_ref[head, :, lower] = low.T
        intra_ref[head, upper] = mm(top, value[upper])
        intra_ref[head, lower] = mm(low, value)
    for copy in copies:
        copy.wait()


def error_kernel(count, first, size, wide_ref, turned_ref, intra_ref, coef_ref, teacher_ref, *refs):
    states, error_ref, adjoint_ref = refs[:count], refs[count], refs[count + 1]
    for head in range(size):
        reads = mm(wide_ref[head], jnp.concatenate([state[head] for state in states], axis=0))
        error = (coef_ref[0] * intra_ref[head] + reads - teacher_ref[first + head].astype(F32)).astype(BF16)
        error_ref[head] = error
        adjoint_ref[head] = mm(turned_ref[head], (coef_ref[count] * error.astype(F32)).astype(BF16)).astype(BF16)


def adjoint_kernel(count, size, turned_ref, coef_ref, error_ref, *adjoints):
    for head in range(size):
        error32 = error_ref[head].astype(F32)
        weighted = [(coef_ref[num + 1] * error32).astype(BF16) for num in range(count - 1)]
        adjoint = mm(turned_ref[head], jnp.concatenate(weighted, axis=1))
        for num in range(count - 1):
            adjoints[num][head] = adjoint[:, num * DK : (num + 1) * DK]


def row_sums(array):
    high = array.astype(BF16)
    ones = jnp.ones((8, DK), BF16)
    return (mm_nt(ones, high) + mm_nt(ones, (array - high.astype(F32)).astype(BF16)))[0:1]


def grad_kernel(gamma, scale_list, count, first, skip, size, query_ref, key_ref, value_ref, error_ref, score_ref, intra_ref, coef_ref, *refs):
    states = refs[:count]
    outq_ref, gk_ref, gv_ref, gl_ref, acc, kept, sems = refs[-7:]
    rows = query_ref.shape[1]
    half = rows // 2
    upper, lower = slice(0, half), slice(half, rows)
    mask = lower_scale(half, gamma)
    copies = []
    for place in range(size):
        head = skip + place
        query, key, value, error = query_ref[first + head], key_ref[head], value_ref[head], error_ref[head]
        error32 = error.astype(F32)
        query32 = query.astype(F32)
        inner = (coef_ref[0] * error32).astype(BF16)
        top = (mask * mm_nt(inner[upper], value[upper])).astype(BF16)
        wide = mm_nt(inner[lower], value)
        left = (gamma * wide[:, upper]).astype(BF16)
        right = (mask * wide[:, lower]).astype(BF16)
        total = jnp.concatenate(
            [mm(top, key[upper]), mm(jnp.concatenate([left, right], axis=1), key)], axis=0
        )
        back = mm_nt(error, jnp.concatenate([state[head] for state in states], axis=0))
        terms = [error32 * intra_ref[head]]
        for num in range(count):
            part = back[:, num * DK : (num + 1) * DK]
            terms.append(query32 * part)
            total += coef_ref[num + 1] * part
        for num, term in enumerate(terms):
            if place == 0:
                acc[num] = term
            else:
                acc[num] += term
        kept[place] = total.astype(BF16)
        copies.append(pltpu.make_async_copy(kept.at[place], outq_ref.at[:, head_columns(first + head)], sems.at[place]))
        copies[-1].start()
        gk_ref[place, upper] = mm_tn(jnp.concatenate([top, left], axis=0), query)
        gk_ref[place, lower] = mm_tn(right, query[lower])
        gv_ref[place, upper] = mm(score_ref[head, upper, :], inner)
        gv_ref[place, lower] = mm(score_ref[head, lower, lower], inner[lower])
    gl_ref[...] = jnp.zeros_like(gl_ref)
    for num, bit in enumerate([1] + level_bits(count)):
        gl_ref[num : num + 1, :] = jnp.where(bit == 1, scale_list[num] * row_sums(acc[num]), 0.0)
    for copy in copies:
        copy.wait()


def final_kernel(count, first, size, pieces, lines, key_ref, value_ref, *refs):
    span = size // pieces
    line_refs, refs = refs[:lines], refs[lines:]
    partk, partv, parts = refs[:pieces], refs[pieces : 2 * pieces], refs[2 * pieces : 2 * pieces + count]
    copies = []
    if lines:
        *refs, line_out, kept_k, kept_v, sems, line_kept, line_sem = refs
        line_kept[...] = sum((part[...] for part in line_refs[1:]), line_refs[0][...])
        copies.append(pltpu.make_async_copy(line_kept, line_out, line_sem))
        copies[0].start()
    else:
        *refs, kept_k, kept_v, sems = refs
    outk_ref, outv_ref = refs[-2:]
    for head in range(size):
        cols = head_columns(first + head)
        total = parts[0][head].astype(F32)
        for part in parts[1:]:
            total += part[head].astype(F32)
        adjoint = total.astype(BF16)
        piece, place = head // span, head % span
        kept_k[head] = (partk[piece][place] + mm_nt(value_ref[head], adjoint)).astype(BF16)
        kept_v[head] = (partv[piece][place] + mm(key_ref[head], adjoint)).astype(BF16)
        for num, (kept, out) in enumerate(((kept_k, outk_ref), (kept_v, outv_ref))):
            copies.append(pltpu.make_async_copy(kept.at[head], out.at[:, cols], sems.at[num, head]))
            copies[-1].start()
    for copy in copies:
        copy.wait()


def on_device(queries, key_rows, value_rows, teacher_out, level_weights):
    rows, width = queries.shape
    heads = width // DK
    inner_count = lax.axis_size("inner")
    outer_count = lax.axis_size("outer")
    inner_bits = inner_count.bit_length() - 1
    outer_bits = outer_count.bit_length() - 1
    count = inner_bits + outer_bits
    gamma = DK ** (-0.5)
    scale_list = [rows ** (-0.5)] + [gamma * (rows * 2 ** (num - 1)) ** (-0.5) for num in range(1, LEVELS)]

    moves = [("inner", 2 ** (bit + 1) - 1) for bit in range(inner_bits)]
    moves += [("outer", 2**bit) for bit in range(outer_bits)]
    size = heads // CHUNKS
    chunks = range(CHUNKS)
    mat = DK * DK
    flop = 2 * rows * mat

    def arr(*shape, dtype=BF16):
        return jax.ShapeDtypeStruct(shape, dtype)

    def params(grant):
        return pltpu.CompilerParams(vmem_limit_bytes=grant * 2**20)

    def state_call(first):
        args, shapes = [key_rows, value_rows], [arr(size, DK, DK), arr(size, rows, DK), arr(size, rows, DK), arr(size, DK, DK)]
        scratch = [pltpu.SemaphoreType.DMA((2, size))]
        if first > 0:
            args.append(queries)
            shapes.append(arr(heads, rows, DK))
            scratch.append(pltpu.SemaphoreType.DMA((heads,)))
        return pl.pallas_call(
            functools.partial(state_kernel, first, size, heads),
            in_specs=[HBM] * len(args),
            out_specs=[VMEM] * len(shapes),
            out_shape=shapes,
            scratch_shapes=scratch,
            compiler_params=params(2),
            cost_estimate=cost(size * flop, size * 4 * rows * DK),
            name="state",
        )(*args)

    def intra_call(first, key, value, earlier):
        shapes = [
            arr(size, rows, rows),
            arr(size, rows, DK, dtype=F32),
            arr(size, DK, rows),
            arr(size, rows, count * DK),
        ]
        if earlier is None:
            args, specs = [key, value, level_weights, query], [VMEM] * 4
            shapes.append(arr(count + 1, rows, DK, dtype=F32))
        else:
            shapes.append(arr(heads, rows, DK))
            args, specs = [key, value, *earlier, teacher_out], [VMEM] * 4 + [HBM]
        return pl.pallas_call(
            functools.partial(intra_kernel, gamma, scale_list, count, first, size, heads, earlier is None),
            in_specs=specs,
            out_specs=[VMEM] * len(shapes),
            out_shape=shapes,
            scratch_shapes=[pltpu.SemaphoreType.DMA((heads,))],
            compiler_params=params(12),
            cost_estimate=cost(size * 12 * flop, size * rows * (6 * DK + 4 * DK + 2 * rows)),
            name="intra",
        )(*args)

    def error_call(first, pre, states):
        _, intra, turned, wide = pre
        return pl.pallas_call(
            functools.partial(error_kernel, count, first, size),
            in_specs=[VMEM] * (5 + count),
            out_specs=[VMEM] * 2,
            out_shape=[arr(size, rows, DK), arr(size, DK, DK)],
            compiler_params=params(8),
            cost_estimate=cost(size * 5 * flop, size * rows * DK * 8),
            name="error",
        )(wide, turned, intra, coef, teacher, *states)

    def adjoint_call(pre, error):
        turned = pre[2]
        return pl.pallas_call(
            functools.partial(adjoint_kernel, count, size),
            in_specs=[VMEM] * 3,
            out_specs=[VMEM] * (count - 1),
            out_shape=[arr(size, DK, DK, dtype=F32)] * (count - 1),
            compiler_params=params(4),
            cost_estimate=cost(size * 3 * flop, size * rows * DK * 6),
            name="adjoint",
        )(turned, coef, error)

    def grad_call(first, skip, span, key, value, pre, states, error, earlier):
        score, intra, _, _ = pre
        args = [query, key, value, error, score, intra, coef, *states]
        specs = [VMEM] * len(args)
        alias = {}
        if earlier is not None:
            alias = {len(args): 0}
            args.append(earlier)
            specs.append(HBM)
        return pl.pallas_call(
            functools.partial(grad_kernel, gamma, scale_list, count, first, skip, span),
            in_specs=specs,
            out_specs=[HBM] + [VMEM] * 3,
            out_shape=[
                arr(rows, width),
                arr(span, rows, DK, dtype=F32),
                arr(span, rows, DK, dtype=F32),
                arr(LEVELS, rows, dtype=F32),
            ],
            scratch_shapes=[
                pltpu.VMEM((count + 1, rows, DK), F32),
                pltpu.VMEM((span, rows, DK), BF16),
                pltpu.SemaphoreType.DMA((span,)),
            ],
            input_output_aliases=alias,
            compiler_params=params(12),
            cost_estimate=cost(span * 24 * flop, span * rows * (24 * DK + 2 * rows)),
            name="grad",
        )(*args)

    def final_call(first, key, value, partk, partv, parts, earlier, lines):
        args = [key, value, *lines, *partk, *partv, *parts]
        specs = [VMEM] * len(args)
        shapes = [arr(rows, width)] * 2
        scratch = [pltpu.VMEM((size, rows, DK), BF16)] * 2 + [pltpu.SemaphoreType.DMA((2, size))]
        alias = {}
        if earlier is not None:
            alias = {len(args) + num: num for num in range(2)}
            args += list(earlier)
            specs += [HBM] * 2
        if lines:
            shapes.append(arr(LEVELS, rows, dtype=F32))
            scratch += [pltpu.VMEM((LEVELS, rows), F32), pltpu.SemaphoreType.DMA]
        return pl.pallas_call(
            functools.partial(final_kernel, count, first, size, len(partk), len(lines)),
            in_specs=specs,
            out_specs=[HBM] * len(shapes),
            out_shape=shapes,
            scratch_shapes=scratch,
            input_output_aliases=alias,
            compiler_params=params(4),
            cost_estimate=cost(size * 2 * flop, size * rows * DK * 16),
            name="final",
        )(*args)

    queries, key_rows, value_rows, teacher_out = [
        pltpu.with_memory_space_constraint(a, pltpu.HBM) for a in (queries, key_rows, value_rows, teacher_out)
    ]
    own, pre = [], []
    for c in chunks:
        own.append(state_call(c * size))
    query = own[1][4]
    for c in chunks:
        early = intra_call(c * size, *own[c][1:3], None if c == 0 else (query, coef))
        pre.append(early[:4])
        if c == 0:
            coef = early[4]
        else:
            teacher = early[4]
    states = [[] for c in chunks]
    for step, (axis, mask) in enumerate(moves):
        for c in chunks:
            sent = own[c][3]
            if step > 0:
                sent = sum((a.astype(F32) for a in states[c]), own[c][0].astype(F32)).astype(BF16)
            states[c].append(swap(sent, axis, mask))
    errors, adjoints = [], []
    for c in chunks:
        error, highest = error_call(c * size, pre[c], states[c])
        errors.append(error)
        adjoints.append((*adjoint_call(pre[c], error), highest))
    parts = [[] for c in chunks]
    for num in reversed(range(count)):
        axis, mask = moves[num]
        for c in chunks:
            running = adjoints[c][num].astype(F32)
            for received in parts[c]:
                running = running + received.astype(F32)
            parts[c].append(swap(running.astype(BF16), axis, mask))
    grad_queries, level_lines, local = None, None, []
    for c in chunks:
        partk, partv = [], []
        span = size // PIECES[c]
        for piece in range(PIECES[c]):
            grad_queries, onek, onev, lines = grad_call(
                c * size, piece * span, span, *own[c][1:3], pre[c], states[c], errors[c], grad_queries
            )
            partk.append(onek)
            partv.append(onev)
            level_lines = lines if level_lines is None else level_lines + lines
        local.append((partk, partv))
    line_parts = [level_lines]
    head_count = lax.axis_size("head")
    for shift in range(1, head_count):
        pairs = [(source, (source + shift) % head_count) for source in range(head_count)]
        line_parts.append(lax.ppermute(level_lines, "head", pairs))
    outs = None
    for c in chunks:
        last = line_parts if c == CHUNKS - 1 else []
        outs = final_call(c * size, *own[c][1:3], *local[c], parts[c], outs, last)
    return (grad_queries, *outs)


def solution(mesh):
    rows = P(("outer", "inner"), "head")
    level = P(None, ("outer", "inner"))
    return jax.shard_map(
        on_device,
        mesh=mesh,
        in_specs=(rows, rows, rows, rows, level),
        out_specs=(rows, rows, rows, level),
        check_vma=False,
    )
```
